32 devices in a mesh: row: 4 (over y, x), col: 4 (over z), depth: 2 (over core).
Axes of the slice: x: 2, y: 2, z: 4, core: 2. Of those that a mesh axis runs over, the one named last changes fastest.
Arguments:
- values: bfloat16 [800, 20, 128, 128], P(('row', 'depth'), 'col'), may hold values from -2 to 2
- pattern: int32 [800, 20], P(('row', 'depth'), 'col'), may hold values from 0 to 199, as said below
- branch_flag: int32 [40], replicated, may hold values from 0 to 1, as said below
Outputs:
- purified: bfloat16 [40, 20, 128, 128], P(('row', 'depth'), 'col')
The draws below stay inside these ranges and needn't reach their ends.
Inputs may be any that keep to these rules, and one draw needn't show every extreme that they name: `pattern`: block columns fall into classes with 5 members in every column panel; block (i, j) is nonzero exactly when i and j are in the same class, and the 5 slots of a block row in panel c list, in no particular order, the distinct panel-local indices of the members of its class in that panel. `branch_flag`: exactly half of the entries, rounded down, are 1; the rest are 0.
All inputs are finite; a program needn't handle non-finite values.
Results may differ from the reference program's by a relative error of at most 0.001.
Values may be sent and summed in bfloat16 or wider, within the bound.
No kernel may reach another device: no remote copies, remote signals or barrier semaphores. Data moves between devices by JAX's collectives and lax.ppermute only.
A program may use at most 128 MiB of HBM per device.

```python
import jax
import jax.numpy as jnp
from jax import lax

NB = 800
BS = 128
WL = 5
PANELS = 4
PANEL_COLS = 200
SLAB = 40
STRIDE = 20
N_COL = 4


def draw_pattern(key, part):
    panel_cols = NB // N_COL
    classes = panel_cols // WL
    subkeys = jax.random.split(jax.random.fold_in(key, 7), N_COL)

    def shuffle(subkey):
        return jax.random.permutation(subkey, panel_cols).astype(jnp.int32)
    orders = jax.vmap(shuffle)(subkeys)
    inverse = jnp.argsort(orders, axis=1).astype(jnp.int32)
    labels = (orders % classes).reshape(NB)
    wanted = labels[:, None, None] + classes * jnp.arange(WL, dtype=jnp.int32)[None, None, :]
    panel_index = jnp.arange(N_COL, dtype=jnp.int32)[None, :, None]
    picked = inverse[panel_index, wanted]
    return picked.reshape(NB, N_COL * WL).astype(jnp.int32)


def draw_branch_flag(key, part):
    order = jax.random.permutation(jax.random.fold_in(key, 11), SLAB).astype(jnp.int32)
    return (order % 2).astype(jnp.int32)


def level_of(stream_key, shape, cuts, low, top_value):
    gain, own = 1.0, jax.random.fold_in(stream_key, 6)
    for axis_at, blocks in cuts:
        heights = jnp.exp(jax.random.uniform(jax.random.fold_in(own, axis_at), (blocks,), jnp.float32, low / len(cuts), top_value / len(cuts)))
        gain = gain * jnp.repeat(heights, shape[axis_at] // blocks).reshape([-1 if axis == axis_at else 1 for axis in range(len(shape))])
    return gain


def bell_draw(stream_key, extent, scale, bound, pieces=(), kind=jnp.bfloat16):
    factor_of = level_of(stream_key, extent, pieces, -0.22, 0.18) if pieces else 1.0
    drawn = jax.random.normal(stream_key, extent, jnp.float32) * scale * factor_of
    return jnp.minimum(jnp.maximum(drawn, -bound), bound).astype(kind)


def setup_inputs(seed: int = 0) -> dict:
    streams_of = jax.random.split(jax.random.key(seed), 4)
    values = bell_draw(streams_of[0], (NB, PANELS * WL, BS, BS), 0.125, 2.0, ((0, 8), (1, 4)))
    pattern = draw_pattern(jax.random.fold_in(streams_of[3], 71), 0)
    branch_flag = draw_branch_flag(jax.random.fold_in(streams_of[3], 71), 0)
    return {"values": values, "pattern": pattern, "branch_flag": branch_flag}


def reference(values, pattern, branch_flag):
    slot_total = PANELS * WL
    panel_of = (jnp.arange(slot_total, dtype=jnp.int32) // WL).astype(jnp.int32)
    slab_rows = (jnp.arange(SLAB, dtype=jnp.int32) * STRIDE).astype(jnp.int32)

    def one_row(items):
        row_index, flag = items
        columns = pattern[row_index]
        inner = (panel_of * PANEL_COLS + columns).astype(jnp.int32)
        right = pattern[inner].reshape(slot_total, PANELS, WL)
        target = columns.reshape(PANELS, WL)
        match = right[:, :, None, :] == target[None, :, :, None]
        present = jnp.any(match, axis=3)
        slot_iota = lax.broadcasted_iota(jnp.int32, match.shape, 3)
        chosen = jnp.sum(jnp.where(match, slot_iota, 0), axis=3).astype(jnp.int32)
        panel_iota = lax.broadcasted_iota(jnp.int32, chosen.shape, 1)
        slot_index = (panel_iota * WL + chosen).reshape(slot_total, slot_total).astype(jnp.int32)
        picked = values[inner[:, None], slot_index]
        picked = jnp.where(present.reshape(slot_total, slot_total)[:, :, None, None], picked, jnp.zeros((), picked.dtype))
        left = values[row_index]
        square = jnp.einsum('lab,lqbc->qac', left.astype(jnp.float32), picked.astype(jnp.float32))
        own = values[row_index].astype(jnp.float32)
        result = jnp.where(flag == 1, square, 2.0 * own - square)
        return result.astype(jnp.bfloat16)

    return lax.map(one_row, (slab_rows, branch_flag))
```

```python
import functools

import jax
import jax.numpy as jnp
from jax import lax
from jax.experimental import pallas as pl
from jax.experimental.pallas import tpu as pltpu
from jax.sharding import PartitionSpec as P


PARTS = (1,)
TOP = 32767.0
MANT = 8192.0


def chunks_of(count):
    total = sum(PARTS)
    edges = [round(count * sum(PARTS[:i]) / total) for i in range(len(PARTS) + 1)]
    return [(a, b - a) for a, b in zip(edges[:-1], edges[1:]) if b > a]


def encode(out_ref, blocks):
    size = blocks[0].shape[0]
    count = len(blocks)
    exps, mants = [], []
    for m, x in enumerate(blocks):
        top = jnp.maximum(jnp.max(jnp.abs(x), axis=0, keepdims=True), 1e-30)
        e = jnp.floor(jnp.log2(top))
        mant = jnp.ceil(top * jnp.exp2(-e) * MANT) + 1.0
        inv = (TOP * MANT) / (mant * jnp.exp2(e))
        q = jnp.clip(jnp.round(x * inv), -TOP, TOP)
        out_ref[pl.ds(m * size, size), :] = q.astype(jnp.int32).astype(jnp.int16)
        exps.append(e)
        mants.append(mant)
    pad = out_ref.shape[0] - count * size - 2 * count
    codes = jnp.concatenate(
        exps + mants + [jnp.zeros((pad, size), jnp.float32)], axis=0
    )
    out_ref[pl.ds(count * size, 2 * count + pad), :] = codes.astype(jnp.int32).astype(jnp.int16)


def scales(ref, count, size):
    codes = ref[count * size :, :].astype(jnp.int32).astype(jnp.float32)
    exps, mants = codes[:count], codes[count : 2 * count]
    return mants * jnp.exp2(exps) * (1.0 / (TOP * MANT))


def decode(ref, scale, m, size):
    q = ref[pl.ds(m * size, size), :].astype(jnp.int32).astype(jnp.float32)
    return q * scale[m : m + 1, :]


def code_rows(count, size):
    return count * size + -(-2 * count // 16) * 16


def gather_panels(values, ups, downs, z, first, n, stride, parts, panels_per_part):
    slots, size = values.shape[1], values.shape[2]
    sources = [values, *ups, *downs]
    offsets = [0] + [-(s + 1) for s in range(len(ups))] + [s + 1 for s in range(len(downs))]

    def index_of(k):
        def index(p, j, i, z_ref):
            q = p * panels_per_part + j
            mine = z_ref[0] + offsets[k]
            step = jnp.where(q == mine, i, jnp.where(q < mine, 0, n - 1))
            if k == 0:
                step = (first + step) * stride
            return (step, 0, 0, 0)
        return index

    def kernel(z_ref, *refs):
        out_ref = refs[-1]
        q = pl.program_id(0) * panels_per_part + pl.program_id(1)
        for k in range(len(sources)):
            @pl.when(q == z_ref[0] + offsets[k])
            def _(k=k):
                out_ref[0, 0, 0] = refs[k][0]

    return pl.pallas_call(
        kernel,
        out_shape=jax.ShapeDtypeStruct((parts, n, panels_per_part, slots, size, size), values.dtype),
        grid_spec=pltpu.PrefetchScalarGridSpec(
            num_scalar_prefetch=1,
            grid=(parts, panels_per_part, n),
            in_specs=[pl.BlockSpec((1, slots, size, size), index_of(k)) for k in range(len(sources))],
            out_specs=pl.BlockSpec(
                (1, 1, 1, slots, size, size), lambda p, j, i, z_ref: (p, i, j, 0, 0, 0)
            ),
        ),
        name="gather_panels",
    )(z.reshape(1), *sources)


def product(lefts, values, table, extra=None):
    rows, terms, size, _ = lefts.shape
    slots = values.shape[1]
    height = code_rows(slots, size)
    krow, keep, slot = table

    def kernel(krow_ref, keep_ref, slot_ref, left_ref, *refs):
        rights, rest = refs[:terms], refs[terms:]
        out_ref = rest[-1]
        i = pl.program_id(0)
        left, right = [], []
        for l in range(terms):
            on = keep_ref[i * terms + l] != 0
            block = left_ref[0, l]
            left.append(jnp.where(on, block, jnp.zeros_like(block)))
            base = (i * terms + l) * slots
            right.append(
                jnp.concatenate([rights[l][0, slot_ref[base + m]] for m in range(slots)], axis=1)
            )
        acc = jnp.dot(
            jnp.concatenate(left, axis=1),
            jnp.concatenate(right, axis=0),
            preferred_element_type=jnp.float32,
        )
        blocks = [acc[:, m * size : (m + 1) * size] for m in range(slots)]
        if extra is not None:
            scale = scales(rest[0].at[0], slots, size)
            blocks = [b + decode(rest[0].at[0], scale, m, size) for m, b in enumerate(blocks)]
        encode(out_ref.at[0], blocks)

    def right_spec(l):
        return pl.BlockSpec(
            (1, slots, size, size), lambda i, krow_ref, *_: (krow_ref[i * terms + l], 0, 0, 0)
        )

    in_specs = [pl.BlockSpec((1, terms, size, size), lambda i, *_: (i, 0, 0, 0))]
    in_specs += [right_spec(l) for l in range(terms)]
    operands = [lefts] + [values] * terms
    if extra is not None:
        in_specs.append(pl.BlockSpec((1, height, size), lambda i, *_: (i, 0, 0)))
        operands.append(extra)
    return pl.pallas_call(
        kernel,
        out_shape=jax.ShapeDtypeStruct((rows, height, size), jnp.int16),
        grid_spec=pltpu.PrefetchScalarGridSpec(
            num_scalar_prefetch=3,
            grid=(rows,),
            in_specs=in_specs,
            out_specs=pl.BlockSpec((1, height, size), lambda i, *_: (i, 0, 0)),
        ),
        cost_estimate=pl.CostEstimate(
            flops=2 * rows * terms * slots * size**3,
            bytes_accessed=rows * terms * (slots + 1) * size * size * 2,
            transcendentals=0,
        ),
        name="product",
    )(krow, keep, slot, *operands)


def finish(received, values, flags, first, stride):
    parts, n, height, size = received.shape
    slots = values.shape[1]

    def kernel(flag_ref, got_ref, own_ref, out_ref):
        flag = flag_ref[first + pl.program_id(0)]
        scale = [scales(got_ref.at[p, 0], slots, size) for p in range(parts)]
        for m in range(slots):
            total = decode(got_ref.at[0, 0], scale[0], m, size)
            for p in range(1, parts):
                total = total + decode(got_ref.at[p, 0], scale[p], m, size)
            own = own_ref[0, m].astype(jnp.float32)
            out_ref[0, m] = jnp.where(flag == 1, total, 2.0 * own - total).astype(out_ref.dtype)

    return pl.pallas_call(
        kernel,
        out_shape=jax.ShapeDtypeStruct((n, slots, size, size), values.dtype),
        grid_spec=pltpu.PrefetchScalarGridSpec(
            num_scalar_prefetch=1,
            grid=(n,),
            in_specs=[
                pl.BlockSpec((parts, 1, height, size), lambda i, f: (0, i, 0, 0)),
                pl.BlockSpec((1, slots, size, size), lambda i, f: ((first + i) * stride, 0, 0, 0)),
            ],
            out_specs=pl.BlockSpec((1, slots, size, size), lambda i, f: (i, 0, 0, 0)),
        ),
        name="finish",
    )(flags, received, values)


def body(values, pattern, branch_flag):
    parts, depths, panels = lax.axis_size("row"), lax.axis_size("depth"), lax.axis_size("col")
    row, depth, z = lax.axis_index("row"), lax.axis_index("depth"), lax.axis_index("col")
    rows_here, slots, size, _ = values.shape
    count = branch_flag.shape[0] // (parts * depths)
    stride = rows_here // count
    panel_cols = rows_here * parts * depths // panels
    per_part = panels // parts
    terms = per_part * slots
    chunks = chunks_of(count)

    cols = pattern[::stride]
    every = lax.all_to_all(
        jnp.broadcast_to(cols[None], (parts * panels * depths, count, slots)),
        ("row", "col", "depth"), split_axis=0, concat_axis=0, tiled=True,
    ).reshape(parts, panels, depths, count, slots)
    left_cols = lax.dynamic_slice_in_dim(every, row * per_part, per_part, 1)
    shift = (jnp.arange(per_part, dtype=jnp.int32) * panel_cols)[None, :, None, None, None]
    local = (left_cols + shift - depth * rows_here).transpose(2, 0, 3, 1, 4)
    local = local.reshape(depths, parts, count, terms)
    out_cols = lax.dynamic_index_in_dim(every, z, 1, keepdims=False).transpose(1, 0, 2, 3)
    keep = (local >= 0) & (local < rows_here)
    krow = jnp.clip(local, 0, rows_here - 1)
    right_cols = pattern[krow]
    match = right_cols[:, :, :, :, None, :] == out_cols[:, :, :, None, :, None]
    slot = jnp.sum(
        jnp.where(match, lax.broadcasted_iota(jnp.int32, match.shape, 5), 0), axis=5
    )
    slot = jnp.minimum(slot, slots - 1)

    def table_of(d, first, n):
        k = lax.dynamic_index_in_dim(krow, d, 0, keepdims=False)[:, first : first + n]
        on = lax.dynamic_index_in_dim(keep, d, 0, keepdims=False)[:, first : first + n]
        s = lax.dynamic_index_in_dim(slot, d, 0, keepdims=False)[:, first : first + n]
        k, on = k.reshape(parts * n, terms), on.reshape(parts * n, terms)
        at = jnp.arange(parts * n, dtype=jnp.int32)
        last = jnp.max(
            jnp.where((at[None, :, None] <= at[:, None, None]) & on[None], at[None, :, None], 0), axis=1
        )
        k = jnp.sum(jnp.where(last[:, None, :] == at[None, :, None], k[None], 0), axis=1)
        return (
            k.astype(jnp.int32).reshape(-1), on.astype(jnp.int32).reshape(-1),
            s.astype(jnp.int32).reshape(-1),
        )

    flags = lax.dynamic_slice_in_dim(branch_flag, (row * depths + depth) * count, count)

    up = [(i, i + 1) for i in range(panels - 1)]
    down = [(i + 1, i) for i in range(panels - 1)]
    outs = []
    for first, n in chunks:
        own = values[first * stride : (first + n - 1) * stride + 1 : stride]
        u = d = own
        ups, downs = [], []
        for _ in range(panels - 1):
            u, d = lax.ppermute(u, "col", up), lax.ppermute(d, "col", down)
            ups.append(u)
            downs.append(d)
        send = gather_panels(values, ups, downs, z, first, n, stride, parts, per_part)
        got = lax.all_to_all(send, "row", split_axis=0, concat_axis=0, tiled=True)
        lefts = got.reshape(parts * n, terms, size, size)
        extra = None
        for s in range(1, depths):
            theirs = lax.ppermute(
                lefts, "depth", [((i + s) % depths, i) for i in range(depths)]
            )
            part = product(theirs, values, table_of((depth + s) % depths, first, n), extra=None)
            back = lax.ppermute(part, "depth", [(i, (i + s) % depths) for i in range(depths)])
            if extra is None:
                extra = back
            else:
                raise NotImplementedError
        mine = product(lefts, values, table_of(depth, first, n), extra=extra)
        mine = mine.reshape(parts, n, *mine.shape[1:])
        summed = lax.all_to_all(mine, "row", split_axis=0, concat_axis=0, tiled=True)
        outs.append(finish(summed, values, flags, first, stride))
    return outs[0] if len(outs) == 1 else jnp.concatenate(outs, axis=0)


def solution(mesh):
    in_specs = (P(("row", "depth"), "col", None, None), P(("row", "depth"), "col"), P())
    out_specs = P(("row", "depth"), "col", None, None)
    return jax.shard_map(body, mesh=mesh, in_specs=in_specs, out_specs=out_specs, check_vma=False)
```

```python
import jax
import jax.numpy as jnp
from jax import lax
from jax.experimental import pallas as pl
from jax.experimental.pallas import tpu as pltpu
from jax.sharding import PartitionSpec as P


PARTS = (3, 2)
TOP = 32767.0
MANT = 8192.0
HERE = pl.BlockSpec(memory_space=pl.ANY)
SCALARS = pl.BlockSpec(memory_space=pltpu.SMEM)
RIGHT_BYTES = 20 << 20


def chunks_of(count):
    total = sum(PARTS)
    edges = [round(count * sum(PARTS[:i]) / total) for i in range(len(PARTS) + 1)]
    return [(a, b - a) for a, b in zip(edges[:-1], edges[1:]) if b > a]


def code_rows(count, size):
    return count * size + -(-2 * count // 16) * 16


def encode(out_ref, blocks):
    size, count = blocks[0].shape[0], len(blocks)
    top = jnp.concatenate([jnp.max(jnp.abs(x), axis=0, keepdims=True) for x in blocks], axis=0)
    top = jnp.maximum(top, 1e-30)
    e = jnp.floor(jnp.log2(top))
    mant = jnp.ceil(top * jnp.exp2(-e) * MANT) + 1.0
    inv = (TOP * MANT) / (mant * jnp.exp2(e))
    for m, x in enumerate(blocks):
        q = jnp.round(x * inv[m : m + 1])
        out_ref[pl.ds(m * size, size), :] = q.astype(jnp.int32).astype(jnp.int16)
    pad = out_ref.shape[0] - count * size - 2 * count
    codes = jnp.concatenate([e, mant, jnp.zeros((pad, size), jnp.float32)], axis=0)
    out_ref[pl.ds(count * size, 2 * count + pad), :] = codes.astype(jnp.int32).astype(jnp.int16)


def scales(ref, count, size):
    codes = ref[count * size :, :].astype(jnp.int32).astype(jnp.float32)
    exps, mants = codes[:count], codes[count : 2 * count]
    return mants * jnp.exp2(exps) * (1.0 / (TOP * MANT))


def decode(ref, scale, m, size):
    q = ref[pl.ds(m * size, size), :].astype(jnp.int32).astype(jnp.float32)
    return q * scale[m : m + 1, :]


def make_tables(where, every, pattern, sizes, chunks):
    parts, panels, depths, count, slots, rows_here, panel_cols = sizes
    per_part = panels // parts
    terms = per_part * slots
    total = parts * depths * count

    def kernel(where_ref, every_ref, pattern_ref, krow_ref, term_ref, slot_ref, live_ref):
        row, depth, z = where_ref[0], where_ref[1], where_ref[2]
        base = 0
        for s in range(depths):
            d = lax.rem(depth + s, depths)
            for first, n in chunks:
                def one(g, carry, base=base, d=d, first=first, n=n):
                    t, i = lax.div(g, n), lax.rem(g, n)
                    p0 = row ^ t

                    def columns_at(q):
                        return (((p0 * panels + q) * depths + d) * count + first + i) * slots

                    at = base + g
                    target = [every_ref[columns_at(z) + m] for m in range(slots)]
                    for l in range(terms):
                        term_ref[at * terms + l] = 0
                        krow_ref[at * terms + l] = 0
                    live = jnp.int32(0)
                    for l in range(terms):
                        j, m = divmod(l, slots)
                        column = every_ref[columns_at(row * per_part + j) + m]
                        k = column + j * panel_cols - depth * rows_here
                        inside = jnp.logical_and(k >= 0, k < rows_here)

                        @pl.when(inside)
                        def _(k=k, l=l, live=live):
                            term_ref[at * terms + live] = l
                            krow_ref[at * terms + live] = k
                            mine = [pattern_ref[k * slots + x] for x in range(slots)]
                            for m, want in enumerate(target):
                                found = jnp.int32(0)
                                for x in range(1, slots):
                                    found = jnp.where(mine[x] == want, x, found)
                                slot_ref[(at * terms + live) * slots + m] = found

                        live = live + inside.astype(jnp.int32)
                    live_ref[at] = live
                    return carry

                lax.fori_loop(0, parts * n, one, 0)
                base += parts * n

    shapes = [total * terms, total * terms, total * terms * slots, total]
    return pl.pallas_call(
        kernel,
        out_shape=[jax.ShapeDtypeStruct((x,), jnp.int32) for x in shapes],
        in_specs=[SCALARS] * 3,
        out_specs=[SCALARS] * 4,
        name="tables",
    )(where, every, pattern)


def gather_panels(own, ups, downs, where, parts, per_part):
    n, slots, size, _ = own.shape
    sources = [own, *ups, *downs]
    offsets = [0] + [-(s + 1) for s in range(len(ups))] + [s + 1 for s in range(len(downs))]

    def kernel(where_ref, *refs):
        outs = refs[len(sources) : len(sources) + parts]
        held, into, outof = refs[len(sources) + parts :]
        row, z = where_ref[0], where_ref[2]
        order = list(range(parts - 1, -1, -1))
        for t in order:
            for j in range(per_part):
                q = (row ^ t) * per_part + j
                for k, offset in enumerate(offsets):
                    @pl.when(q == z + offset)
                    def _(t=t, j=j, k=k):
                        to = t * per_part + j
                        pltpu.make_async_copy(refs[k], held.at[to], into.at[to]).start()
        copies = []
        for t in order:
            for j in range(per_part):
                to = t * per_part + j
                pltpu.make_async_copy(refs[0], held.at[to], into.at[to]).wait()
                copies.append(
                    pltpu.make_async_copy(
                        held.at[to], outs[t].at[:, pl.ds(j * slots, slots)], outof.at[to]
                    )
                )
                copies[-1].start()
        for copy in copies:
            copy.wait()

    panels = parts * per_part
    out = jax.ShapeDtypeStruct((n, per_part * slots, size, size), own.dtype)
    return pl.pallas_call(
        kernel,
        out_shape=[out] * parts,
        in_specs=[SCALARS] + [HERE] * len(sources),
        out_specs=[HERE] * parts,
        scratch_shapes=[
            pltpu.VMEM((panels, n, slots, size, size), own.dtype),
            pltpu.SemaphoreType.DMA((panels,)),
            pltpu.SemaphoreType.DMA((panels,)),
        ],
        cost_estimate=pl.CostEstimate(
            flops=0, bytes_accessed=4 * panels * n * slots * size * size, transcendentals=0
        ),
        name="gather_panels",
    )(where, *sources)


def product(lefts, values, tables, base, extra=None, joined=False):
    parts = len(lefts)
    n, terms, size, _ = lefts[0].shape
    slots = values.shape[1]
    height = code_rows(slots, size)
    rows = parts * n
    ahead = max(2, min(rows, RIGHT_BYTES // (terms * slots * size * size * 2)))

    def kernel(krow_ref, term_ref, slot_ref, live_ref, values_ref, *refs):
        left_refs, rest = refs[:parts], refs[parts:]
        if extra is not None:
            extra_ref, rest = rest[0], rest[1:]
        outs = rest[: 1 if joined else parts]
        left, right, acc, coded, got, left_sem, right_sem, got_sem, out_sem = rest[len(outs) :]

        def rights(g, act):
            at = lax.rem(g, ahead)
            for l in range(terms):
                @pl.when(l < live_ref[base + g])
                def _(l=l):
                    k = krow_ref[(base + g) * terms + l]
                    act(pltpu.make_async_copy(values_ref.at[k], right.at[at, l], right_sem.at[at, l]))

        def left_copy(t):
            return pltpu.make_async_copy(left_refs[t], left.at[pl.ds(t * n, n)], left_sem.at[t])

        def got_copy(t):
            part = pl.ds(t * n, n)
            return pltpu.make_async_copy(extra_ref.at[part], got.at[part], got_sem.at[t])

        def out_copy(t):
            part = pl.ds(t * n, n)
            to = outs[0].at[part] if joined else outs[t]
            return pltpu.make_async_copy(coded.at[part], to, out_sem.at[t])

        for t in range(parts):
            left_copy(t).start()
            if extra is not None:
                got_copy(t).start()

        def prime(g, carry):
            rights(g, lambda copy: copy.start())
            return carry

        lax.fori_loop(0, ahead - 1 if ahead < rows else rows, prime, 0)

        def one(g, carry):
            if ahead < rows:
                @pl.when(g + ahead - 1 < rows)
                def _():
                    rights(g + ahead - 1, lambda copy: copy.start())
            for t in range(parts):
                @pl.when(g == t * n)
                def _(t=t):
                    left_copy(t).wait()
                    if extra is not None:
                        got_copy(t).wait()
            rights(g, lambda copy: copy.wait())
            live = live_ref[base + g]
            at = lax.rem(g, ahead)

            def dot_of(low, number):
                sides = []
                for l in range(low, low + number):
                    entry = (base + g) * terms + l
                    sides.append(
                        (
                            left[g, term_ref[entry]],
                            jnp.concatenate(
                                [right[at, l, slot_ref[entry * slots + m]] for m in range(slots)], axis=1
                            ),
                        )
                    )
                return jnp.dot(
                    jnp.concatenate([a for a, _ in sides], axis=1),
                    jnp.concatenate([b for _, b in sides], axis=0),
                    preferred_element_type=jnp.float32,
                )

            @pl.when(live == 0)
            def _():
                acc[...] = jnp.zeros_like(acc)

            for low in range(0, terms, 2):
                for number in (1, 2):
                    if low + number > terms:
                        continue

                    @pl.when(live == low + 1 if number == 1 else live >= low + 2)
                    def _(low=low, number=number):
                        if low == 0:
                            acc[...] = dot_of(low, number)
                        else:
                            acc[...] += dot_of(low, number)

            blocks = [acc[:, m * size : (m + 1) * size] for m in range(slots)]
            if extra is not None:
                scale = scales(got.at[g], slots, size)
                blocks = [b + decode(got.at[g], scale, m, size) for m, b in enumerate(blocks)]
            encode(coded.at[g], blocks)
            for t in range(parts):
                @pl.when(g == t * n + n - 1)
                def _(t=t):
                    out_copy(t).start()
            return carry

        lax.fori_loop(0, rows, one, 0)
        for t in range(parts):
            out_copy(t).wait()

    if joined:
        out_shape = [jax.ShapeDtypeStruct((rows, height, size), jnp.int16)]
    else:
        out_shape = [jax.ShapeDtypeStruct((n, height, size), jnp.int16)] * parts
    operands = [*tables, values, *lefts] + ([] if extra is None else [extra])
    dma = pltpu.SemaphoreType.DMA
    got_rows = rows if extra is not None else 1
    out = pl.pallas_call(
        kernel,
        out_shape=out_shape,
        in_specs=[SCALARS] * 4 + [HERE] * (len(operands) - 4),
        out_specs=[HERE] * len(out_shape),
        scratch_shapes=[
            pltpu.VMEM((rows, terms, size, size), values.dtype),
            pltpu.VMEM((ahead, terms, slots, size, size), values.dtype),
            pltpu.VMEM((size, slots * size), jnp.float32),
            pltpu.VMEM((rows, height, size), jnp.int16),
            pltpu.VMEM((got_rows, height, size), jnp.int16),
            dma((parts,)), dma((ahead, terms)), dma((parts,)), dma((parts,)),
        ],
        cost_estimate=pl.CostEstimate(
            flops=2 * rows * terms * slots * size**3,
            bytes_accessed=rows * terms * (slots + 1) * size * size * 2,
            transcendentals=0,
        ),
        name="product",
    )(*operands)
    return out[0] if joined else out


def finish(received, values, flags, first, stride, count, before=None):
    parts = len(received)
    n, height, size = received[0].shape
    slots = values.shape[1]

    def kernel(flag_ref, own_ref, *refs):
        got, out_ref = refs[:parts], refs[-1]
        flag = flag_ref[first + pl.program_id(0)]
        scale = [scales(g.at[0], slots, size) for g in got]
        for m in range(slots):
            total = decode(got[0].at[0], scale[0], m, size)
            for p in range(1, parts):
                total = total + decode(got[p].at[0], scale[p], m, size)
            own = own_ref[0, m].astype(jnp.float32)
            out_ref[0, m] = jnp.where(flag == 1, total, 2.0 * own - total).astype(out_ref.dtype)

    piece = pl.BlockSpec((1, height, size), lambda i, f: (i, 0, 0))
    in_specs = [pl.BlockSpec((1, slots, size, size), lambda i, f: ((first + i) * stride, 0, 0, 0))]
    in_specs += [piece] * parts
    operands = [flags, values, *received]
    if before is not None:
        in_specs.append(HERE)
        operands.append(before)
    return pl.pallas_call(
        kernel,
        out_shape=jax.ShapeDtypeStruct((count, slots, size, size), values.dtype),
        grid_spec=pltpu.PrefetchScalarGridSpec(
            num_scalar_prefetch=1,
            grid=(n,),
            in_specs=in_specs,
            out_specs=pl.BlockSpec((1, slots, size, size), lambda i, f: (first + i, 0, 0, 0)),
        ),
        input_output_aliases={} if before is None else {len(operands) - 1: 0},
        name="finish",
    )(*operands)


def inner(values, pattern, branch_flag):
    parts, depths, panels = lax.axis_size("row"), lax.axis_size("depth"), lax.axis_size("col")
    row, depth, z = lax.axis_index("row"), lax.axis_index("depth"), lax.axis_index("col")
    rows_here, slots, _, _ = values.shape
    count = branch_flag.shape[0] // (parts * depths)
    stride = rows_here // count
    panel_cols = rows_here * parts * depths // panels
    per_part = panels // parts
    chunks = chunks_of(count)
    across = [[(i, i ^ t) for i in range(parts)] for t in range(parts)]
    up = [(i, i + 1) for i in range(panels - 1)]
    down = [(i + 1, i) for i in range(panels - 1)]
    where = jnp.stack([row, depth, z]).astype(jnp.int32)

    own = [values[a * stride : (a + n - 1) * stride + 1 : stride] for a, n in chunks]
    ups, downs = [[] for _ in chunks], [[] for _ in chunks]
    u, d = list(own), list(own)
    every = lax.all_to_all(
        jnp.broadcast_to(pattern[None, ::stride], (parts * panels * depths, count, slots)),
        ("row", "col", "depth"), split_axis=0, concat_axis=0, tiled=True,
    )
    tables = make_tables(
        where, every.reshape(-1), pattern.reshape(-1),
        (parts, panels, depths, count, slots, rows_here, panel_cols), chunks,
    )
    flags = lax.dynamic_slice_in_dim(branch_flag, (row * depths + depth) * count, count)

    for _ in range(panels - 1):
        for c in range(len(chunks)):
            u[c] = lax.ppermute(u[c], "col", up)
            d[c] = lax.ppermute(d[c], "col", down)
            ups[c].append(u[c])
            downs[c].append(d[c])

    out = None
    lefts = []
    for c in range(len(chunks)):
        picked = gather_panels(own[c], ups[c], downs[c], where, parts, per_part)
        got = [picked[0]]
        for t in range(1, parts):
            got.append(lax.ppermute(picked[t], "row", across[t]))
        lefts.append(got)

    base = [sum(parts * m for _, m in chunks[:c]) for c in range(len(chunks))]
    per_depth = parts * count
    for c, (first, n) in enumerate(chunks):
        extra = None
        for s in range(1, depths):
            here = []
            for t in range(parts):
                here.append(
                    lax.ppermute(lefts[c][t], "depth", [((i + s) % depths, i) for i in range(depths)])
                )
            part = product(here, values, tables, s * per_depth + base[c], joined=True)
            back = lax.ppermute(part, "depth", [(i, (i + s) % depths) for i in range(depths)])
            assert extra is None
            extra = back
        mine = product(lefts[c], values, tables, base[c], extra=extra)
        summed = [mine[0]]
        for t in range(1, parts):
            summed.append(lax.ppermute(mine[t], "row", across[t]))
        out = finish(summed, values, flags, first, stride, count, before=out)
    return out


def solution(mesh):
    in_specs = (P(("row", "depth"), "col", None, None), P(("row", "depth"), "col"), P())
    out_specs = P(("row", "depth"), "col", None, None)
    return jax.shard_map(inner, mesh=mesh, in_specs=in_specs, out_specs=out_specs, check_vma=False)
```

```python
import jax
import jax.numpy as jnp
from jax import lax
from jax.experimental import pallas as pl
from jax.experimental.pallas import tpu as pltpu
from jax.sharding import PartitionSpec as P


PARTS = (2, 2, 1)
TOP = 32767.0
MANT = 8192.0
HERE = pl.BlockSpec(memory_space=pltpu.HBM)
SCALARS = pl.BlockSpec(memory_space=pltpu.SMEM)
NEAR = pl.BlockSpec(memory_space=pltpu.VMEM)
VMEM_BYTES = 8 << 20


def chunks_of(count):
    total = sum(PARTS)
    edges = [round(count * sum(PARTS[:i]) / total) for i in range(len(PARTS) + 1)]
    return [(a, b - a) for a, b in zip(edges[:-1], edges[1:]) if b > a]


def code_rows(count, size):
    return count * size + -(-2 * count // 16) * 16


def encode(out_ref, blocks):
    size, count = blocks[0].shape[0], len(blocks)
    top = jnp.concatenate([jnp.max(jnp.abs(x), axis=0, keepdims=True) for x in blocks], axis=0)
    top = jnp.maximum(top, 1e-30)
    e = jnp.floor(jnp.log2(top))
    mant = jnp.ceil(top * jnp.exp2(-e) * MANT) + 1.0
    inv = (TOP * MANT) / (mant * jnp.exp2(e))
    for m, x in enumerate(blocks):
        q = jnp.round(x * inv[m : m + 1])
        out_ref[pl.ds(m * size, size), :] = q.astype(jnp.int32).astype(jnp.int16)
    pad = out_ref.shape[0] - count * size - 2 * count
    codes = jnp.concatenate([e, mant, jnp.zeros((pad, size), jnp.float32)], axis=0)
    out_ref[pl.ds(count * size, 2 * count + pad), :] = codes.astype(jnp.int32).astype(jnp.int16)


def scales(ref, count, size):
    codes = ref[count * size :, :].astype(jnp.int32).astype(jnp.float32)
    exps, mants = codes[:count], codes[count : 2 * count]
    return mants * jnp.exp2(exps) * (1.0 / (TOP * MANT))


def decode(ref, scale, m, size):
    q = ref[pl.ds(m * size, size), :].astype(jnp.int32).astype(jnp.float32)
    return q * scale[m : m + 1, :]


def record_size(terms, slots):
    return 1 + 2 * terms + terms * slots


def make_tables(where, every, pattern, sizes, chunks):
    parts, panels, depths, count, slots, rows_here, panel_cols = sizes
    per_part = panels // parts
    terms = per_part * slots
    total, record = parts * depths * count, record_size(terms, slots)

    def kernel(where_ref, every_ref, pattern_ref, out_ref):
        row, depth, z = where_ref[0], where_ref[1], where_ref[2]
        base = 0
        for s in range(depths):
            d = lax.rem(depth + s, depths)
            for first, n in chunks:
                def one(g, carry, base=base, d=d, first=first, n=n):
                    t, i = lax.div(g, n), lax.rem(g, n)
                    p0 = row ^ t

                    def columns_at(q):
                        return (((p0 * panels + q) * depths + d) * count + first + i) * slots

                    at = (base + g) * record
                    target = [every_ref[columns_at(z) + m] for m in range(slots)]
                    live = jnp.int32(0)
                    for l in range(terms):
                        j, m = divmod(l, slots)
                        column = every_ref[columns_at(row * per_part + j) + m]
                        k = column + j * panel_cols - depth * rows_here
                        inside = jnp.logical_and(k >= 0, k < rows_here)

                        @pl.when(inside)
                        def _(k=k, l=l, live=live):
                            out_ref[at + 1 + live] = l
                            out_ref[at + 1 + terms + live] = k
                            mine = [pattern_ref[k * slots + x] for x in range(slots)]
                            for m, want in enumerate(target):
                                found = jnp.int32(0)
                                for x in range(1, slots):
                                    found = jnp.where(mine[x] == want, x, found)
                                out_ref[at + 1 + 2 * terms + live * slots + m] = found

                        live = live + inside.astype(jnp.int32)
                    out_ref[at] = live
                    return carry

                lax.fori_loop(0, parts * n, one, 0)
                base += parts * n

    return pl.pallas_call(
        kernel,
        out_shape=jax.ShapeDtypeStruct((total * record,), jnp.int32),
        in_specs=[SCALARS] * 3,
        out_specs=SCALARS,
        compiler_params=pltpu.CompilerParams(vmem_limit_bytes=VMEM_BYTES),
        name="tables",
    )(where, every, pattern)


def bring(values):
    rows = values.shape[0]
    cuts = [rows * i // 4 for i in range(5)]

    def kernel(values_ref, out_ref, sem):
        copies = []
        for i, (a, b) in enumerate(zip(cuts[:-1], cuts[1:])):
            part = pl.ds(a, b - a)
            copies.append(pltpu.make_async_copy(values_ref.at[part], out_ref.at[part], sem.at[i]))
            copies[-1].start()
        for copy in copies:
            copy.wait()

    return pl.pallas_call(
        kernel,
        out_shape=jax.ShapeDtypeStruct(values.shape, values.dtype),
        in_specs=[HERE],
        out_specs=NEAR,
        scratch_shapes=[pltpu.SemaphoreType.DMA((4,))],
        compiler_params=pltpu.CompilerParams(vmem_limit_bytes=4 * VMEM_BYTES),
        name="bring",
    )(values)


def gather_panels(sources, where, parts, per_part):
    n, slots, size, _ = sources[0].shape
    ring = len(sources)

    def kernel(where_ref, *refs):
        outs, sem = refs[len(sources) : len(sources) + parts], refs[-1]
        row, z = where_ref[0], where_ref[2]
        places = [(t, j) for t in range(parts - 1, -1, -1) for j in range(per_part)]

        def copy(k, t, j):
            to = outs[t].at[:, pl.ds(j * slots, slots)]
            return pltpu.make_async_copy(refs[k], to, sem.at[t * per_part + j])

        for t, j in places:
            q = (row ^ t) * per_part + j
            for k in range(ring):
                @pl.when(q == lax.rem(z + ring - k, ring))
                def _(t=t, j=j, k=k):
                    copy(k, t, j).start()
        for t, j in places:
            copy(0, t, j).wait()

    panels = parts * per_part
    out = jax.ShapeDtypeStruct((n, per_part * slots, size, size), sources[0].dtype)
    return pl.pallas_call(
        kernel,
        out_shape=[out] * parts,
        in_specs=[SCALARS] + [NEAR] * len(sources),
        out_specs=[NEAR] * parts,
        scratch_shapes=[pltpu.SemaphoreType.DMA((panels,))],
        compiler_params=pltpu.CompilerParams(vmem_limit_bytes=VMEM_BYTES),
        cost_estimate=pl.CostEstimate(
            flops=0, bytes_accessed=4 * panels * n * slots * size * size, transcendentals=0
        ),
        name="gather_panels",
    )(where, *sources)


def product(lefts, values, table, base, extra=None, joined=False):
    parts = len(lefts)
    n, terms, size, _ = lefts[0].shape
    slots = values.shape[1]
    height = code_rows(slots, size)
    rows, record = parts * n, record_size(terms, slots)

    def kernel(table_ref, values_ref, *refs):
        left_refs, rest = refs[:parts], refs[parts:]
        if extra is not None:
            extra_ref, rest = rest[0], rest[1:]
        outs, acc = rest[:-1], rest[-1]

        for t in range(parts):
            def one(i, carry, t=t):
                g = t * n + i
                at = (base + g) * record
                live = table_ref[at]

                def dot_of(low, number):
                    left, right = [], []
                    for l in range(low, low + number):
                        k = table_ref[at + 1 + terms + l]
                        slot = at + 1 + 2 * terms + l * slots
                        left.append(left_refs[t][i, table_ref[at + 1 + l]])
                        right.append(
                            jnp.concatenate(
                                [values_ref[k, table_ref[slot + m]] for m in range(slots)], axis=1
                            )
                        )
                    return jnp.dot(
                        jnp.concatenate(left, axis=1),
                        jnp.concatenate(right, axis=0),
                        preferred_element_type=jnp.float32,
                    )

                @pl.when(live == 0)
                def _():
                    acc[...] = jnp.zeros_like(acc)

                for low in range(0, terms, 2):
                    for number in (1, 2):
                        if low + number > terms:
                            continue

                        @pl.when(live == low + 1 if number == 1 else live >= low + 2)
                        def _(low=low, number=number):
                            if low == 0:
                                acc[...] = dot_of(low, number)
                            else:
                                acc[...] += dot_of(low, number)

                blocks = [acc[:, m * size : (m + 1) * size] for m in range(slots)]
                if extra is not None:
                    scale = scales(extra_ref.at[g], slots, size)
                    blocks = [b + decode(extra_ref.at[g], scale, m, size) for m, b in enumerate(blocks)]
                encode(outs[0].at[g] if joined else outs[t].at[i], blocks)
                return carry

            lax.fori_loop(0, n, one, 0)

    if joined:
        out_shape = [jax.ShapeDtypeStruct((rows, height, size), jnp.int16)]
    else:
        out_shape = [jax.ShapeDtypeStruct((n, height, size), jnp.int16)] * parts
    operands = [table, values, *lefts] + ([] if extra is None else [extra])
    out = pl.pallas_call(
        kernel,
        out_shape=out_shape,
        in_specs=[SCALARS] + [NEAR] * (len(operands) - 1),
        out_specs=[NEAR] * len(out_shape),
        scratch_shapes=[pltpu.VMEM((size, slots * size), jnp.float32)],
        compiler_params=pltpu.CompilerParams(vmem_limit_bytes=VMEM_BYTES),
        cost_estimate=pl.CostEstimate(
            flops=2 * rows * terms * slots * size**3,
            bytes_accessed=rows * terms * (slots + 1) * size * size * 2,
            transcendentals=0,
        ),
        name="product",
    )(*operands)
    return out[0] if joined else out


def finish(received, own, flags, where, depths, first, count, before=None):
    parts = len(received)
    n, _, size = received[0].shape
    slots = own.shape[1]

    def kernel(flag_ref, where_ref, own_ref, *refs):
        got, out_ref = refs[:parts], refs[-1]
        i = pl.program_id(0)
        flag = flag_ref[(where_ref[0] * depths + where_ref[1]) * count + first + i]
        scale = [scales(g.at[i], slots, size) for g in got]
        for m in range(slots):
            total = decode(got[0].at[i], scale[0], m, size)
            for p in range(1, parts):
                total = total + decode(got[p].at[i], scale[p], m, size)
            mine = own_ref[i, m].astype(jnp.float32)
            out_ref[0, m] = jnp.where(flag == 1, total, 2.0 * mine - total).astype(out_ref.dtype)

    in_specs = [NEAR] * (parts + 1)
    operands = [flags, where, own, *received]
    if before is not None:
        in_specs.append(HERE)
        operands.append(before)
    return pl.pallas_call(
        kernel,
        out_shape=jax.ShapeDtypeStruct((count, slots, size, size), own.dtype),
        grid_spec=pltpu.PrefetchScalarGridSpec(
            num_scalar_prefetch=2,
            grid=(n,),
            in_specs=in_specs,
            out_specs=pl.BlockSpec((1, slots, size, size), lambda i, *_: (first + i, 0, 0, 0)),
        ),
        compiler_params=pltpu.CompilerParams(vmem_limit_bytes=VMEM_BYTES),
        input_output_aliases={} if before is None else {len(operands) - 1: 0},
        name="finish",
    )(*operands)


def inner(values, pattern, branch_flag):
    parts, depths, panels = lax.axis_size("row"), lax.axis_size("depth"), lax.axis_size("col")
    row, depth, z = lax.axis_index("row"), lax.axis_index("depth"), lax.axis_index("col")
    rows_here, slots, _, _ = values.shape
    count = branch_flag.shape[0] // (parts * depths)
    stride = rows_here // count
    panel_cols = rows_here * parts * depths // panels
    per_part = panels // parts
    chunks = chunks_of(count)
    across = [[(i, i ^ t) for i in range(parts)] for t in range(parts)]
    ring = [(i, (i + 1) % panels) for i in range(panels)]
    where = jnp.stack([row, depth, z]).astype(jnp.int32)

    own = [values[a * stride : (a + n - 1) * stride + 1 : stride] for a, n in chunks]
    every = lax.all_to_all(
        jnp.broadcast_to(pattern[None, ::stride], (parts * panels * depths, count, slots)),
        ("row", "col", "depth"), split_axis=0, concat_axis=0, tiled=True,
    )
    tables = make_tables(
        where, every.reshape(-1), pattern.reshape(-1),
        (parts, panels, depths, count, slots, rows_here, panel_cols), chunks,
    )
    near = bring(values)

    held = [[x] for x in own]
    for _ in range(panels - 1):
        for c in range(len(chunks)):
            held[c].append(lax.ppermute(held[c][-1], "col", ring))

    out = None
    lefts = []
    for c in range(len(chunks)):
        picked = gather_panels(held[c], where, parts, per_part)
        got = [picked[0]]
        for t in range(1, parts):
            got.append(lax.ppermute(picked[t], "row", across[t]))
        lefts.append(got)

    base = [sum(parts * m for _, m in chunks[:c]) for c in range(len(chunks))]
    per_depth = parts * count
    for c, (first, n) in enumerate(chunks):
        extra = None
        for s in range(1, depths):
            here = []
            for t in range(parts):
                here.append(
                    lax.ppermute(lefts[c][t], "depth", [((i + s) % depths, i) for i in range(depths)])
                )
            part = product(here, near, tables, s * per_depth + base[c], joined=True)
            back = lax.ppermute(part, "depth", [(i, (i + s) % depths) for i in range(depths)])
            assert extra is None
            extra = back
        mine = product(lefts[c], near, tables, base[c], extra=extra)
        summed = [mine[0]]
        for t in range(1, parts):
            summed.append(lax.ppermute(mine[t], "row", across[t]))
        out = finish(summed, own[c], branch_flag, where, depths, first, count, before=out)
    return out


def solution(mesh):
    in_specs = (P(("row", "depth"), "col", None, None), P(("row", "depth"), "col"), P())
    out_specs = P(("row", "depth"), "col", None, None)
    return jax.shard_map(inner, mesh=mesh, in_specs=in_specs, out_specs=out_specs, check_vma=False)
```

```python
import jax
import jax.numpy as jnp
from jax import lax
from jax.experimental import pallas as pl
from jax.experimental.pallas import tpu as pltpu
from jax.sharding import PartitionSpec as P


PARTS = (2, 2, 1)
TOP = 32767.0
MANT = 8192.0
HERE = pl.BlockSpec(memory_space=pltpu.HBM)
SCALARS = pl.BlockSpec(memory_space=pltpu.SMEM)
NEAR = pl.BlockSpec(memory_space=pltpu.VMEM)
VMEM_BYTES = 8 << 20


def chunks_of(count):
    total = sum(PARTS)
    edges = [round(count * sum(PARTS[:i]) / total) for i in range(len(PARTS) + 1)]
    return [(a, b - a) for a, b in zip(edges[:-1], edges[1:]) if b > a]


def code_rows(count, size):
    return count * size + -(-2 * count // 16) * 16


def encode(out_ref, blocks):
    size, count = blocks[0].shape[0], len(blocks)
    top = jnp.concatenate([jnp.max(jnp.abs(x), axis=0, keepdims=True) for x in blocks], axis=0)
    top = jnp.maximum(top, 1e-30)
    e = jnp.floor(jnp.log2(top))
    mant = jnp.ceil(top * jnp.exp2(-e) * MANT) + 1.0
    inv = (TOP * MANT) / (mant * jnp.exp2(e))
    for m, x in enumerate(blocks):
        q = jnp.round(x * inv[m : m + 1])
        out_ref[pl.ds(m * size, size), :] = q.astype(jnp.int32).astype(jnp.int16)
    pad = out_ref.shape[0] - count * size - 2 * count
    codes = jnp.concatenate([e, mant, jnp.zeros((pad, size), jnp.float32)], axis=0)
    out_ref[pl.ds(count * size, 2 * count + pad), :] = codes.astype(jnp.int32).astype(jnp.int16)


def scales(ref, count, size):
    codes = ref[count * size :, :].astype(jnp.int32).astype(jnp.float32)
    exps, mants = codes[:count], codes[count : 2 * count]
    return mants * jnp.exp2(exps) * (1.0 / (TOP * MANT))


def decode(ref, scale, m, size):
    q = ref[pl.ds(m * size, size), :].astype(jnp.int32).astype(jnp.float32)
    return q * scale[m : m + 1, :]


def record_size(terms, slots):
    return 1 + 2 * terms + terms * slots


def make_tables(where, every, pattern, values, sizes, chunks):
    parts, panels, depths, count, slots, rows_here, panel_cols = sizes
    per_part = panels // parts
    terms = per_part * slots
    total, record = parts * depths * count, record_size(terms, slots)

    cuts = [rows_here * i // 4 for i in range(5)]

    def kernel(where_ref, every_ref, pattern_ref, values_ref, out_ref, near_ref, sem):
        copies = []
        for i, (a, b) in enumerate(zip(cuts[:-1], cuts[1:])):
            part = pl.ds(a, b - a)
            copies.append(pltpu.make_async_copy(values_ref.at[part], near_ref.at[part], sem.at[i]))
            copies[-1].start()
        row, depth, z = where_ref[0], where_ref[1], where_ref[2]
        base = 0
        for s in range(depths):
            d = lax.rem(depth + s, depths)
            for first, n in chunks:
                def one(g, carry, base=base, d=d, first=first, n=n):
                    t, i = lax.div(g, n), lax.rem(g, n)
                    p0 = row ^ t

                    def columns_at(q):
                        return (((p0 * panels + q) * depths + d) * count + first + i) * slots

                    at = (base + g) * record
                    target = [every_ref[columns_at(z) + m] for m in range(slots)]
                    live = jnp.int32(0)
                    for l in range(terms):
                        j, m = divmod(l, slots)
                        column = every_ref[columns_at(row * per_part + j) + m]
                        k = column + j * panel_cols - depth * rows_here
                        inside = jnp.logical_and(k >= 0, k < rows_here)

                        @pl.when(inside)
                        def _(k=k, l=l, live=live):
                            out_ref[at + 1 + live] = l
                            out_ref[at + 1 + terms + live] = k
                            mine = [pattern_ref[k * slots + x] for x in range(slots)]
                            for m, want in enumerate(target):
                                found = jnp.int32(0)
                                for x in range(1, slots):
                                    found = jnp.where(mine[x] == want, x, found)
                                out_ref[at + 1 + 2 * terms + live * slots + m] = found

                        live = live + inside.astype(jnp.int32)
                    out_ref[at] = live
                    return carry

                lax.fori_loop(0, parts * n, one, 0)
                base += parts * n
        for copy in copies:
            copy.wait()

    return pl.pallas_call(
        kernel,
        out_shape=[
            jax.ShapeDtypeStruct((total * record,), jnp.int32),
            jax.ShapeDtypeStruct(values.shape, values.dtype),
        ],
        in_specs=[SCALARS] * 3 + [HERE],
        out_specs=[SCALARS, NEAR],
        scratch_shapes=[pltpu.SemaphoreType.DMA((4,))],
        compiler_params=pltpu.CompilerParams(vmem_limit_bytes=4 * VMEM_BYTES),
        name="tables",
    )(where, every, pattern, values)


def stop_of(z, panels):
    even = jnp.where(z == 0, 0, panels - lax.div(z, 2))
    return jnp.where(lax.rem(z, 2) == 1, lax.div(z + 1, 2), even)


def gather_panels(sources, where, parts, per_part):
    n, slots, size, _ = sources[0].shape
    ring = len(sources)

    def kernel(where_ref, *refs):
        outs, sem = refs[len(sources) : len(sources) + parts], refs[-1]
        row, z = where_ref[0], where_ref[2]
        here = stop_of(z, ring)
        places = [(t, j) for t in range(parts - 1, -1, -1) for j in range(per_part)]

        def copy(k, t, j):
            to = outs[t].at[:, pl.ds(j * slots, slots)]
            return pltpu.make_async_copy(refs[k], to, sem.at[t * per_part + j])

        for t, j in places:
            q = (row ^ t) * per_part + j
            behind = lax.rem(here - stop_of(q, ring) + ring, ring)
            for k in range(ring):
                @pl.when(behind == k)
                def _(t=t, j=j, k=k):
                    copy(k, t, j).start()
        for t, j in places:
            copy(0, t, j).wait()

    panels = parts * per_part
    out = jax.ShapeDtypeStruct((n, per_part * slots, size, size), sources[0].dtype)
    return pl.pallas_call(
        kernel,
        out_shape=[out] * parts,
        in_specs=[SCALARS] + [NEAR] * len(sources),
        out_specs=[NEAR] * parts,
        scratch_shapes=[pltpu.SemaphoreType.DMA((panels,))],
        compiler_params=pltpu.CompilerParams(vmem_limit_bytes=VMEM_BYTES),
        cost_estimate=pl.CostEstimate(
            flops=0, bytes_accessed=4 * panels * n * slots * size * size, transcendentals=0
        ),
        name="gather_panels",
    )(where, *sources)


def product(lefts, values, table, base, extra=None, joined=False):
    parts = len(lefts)
    n, terms, size, _ = lefts[0].shape
    slots = values.shape[1]
    height = code_rows(slots, size)
    rows, record = parts * n, record_size(terms, slots)

    def kernel(table_ref, values_ref, *refs):
        left_refs, rest = refs[:parts], refs[parts:]
        if extra is not None:
            extra_ref, rest = rest[0], rest[1:]
        outs, acc = rest[:-1], rest[-1]

        for t in range(parts):
            def one(i, carry, t=t):
                g = t * n + i
                at = (base + g) * record
                live = table_ref[at]

                def dot_of(low, number):
                    left, right = [], []
                    for l in range(low, low + number):
                        k = table_ref[at + 1 + terms + l]
                        slot = at + 1 + 2 * terms + l * slots
                        left.append(left_refs[t][i, table_ref[at + 1 + l]])
                        right.append(
                            jnp.concatenate(
                                [values_ref[k, table_ref[slot + m]] for m in range(slots)], axis=1
                            )
                        )
                    return jnp.dot(
                        jnp.concatenate(left, axis=1),
                        jnp.concatenate(right, axis=0),
                        preferred_element_type=jnp.float32,
                    )

                @pl.when(live == 0)
                def _():
                    acc[...] = jnp.zeros_like(acc)

                for low in range(0, terms, 2):
                    for number in (1, 2):
                        if low + number > terms:
                            continue

                        @pl.when(live == low + 1 if number == 1 else live >= low + 2)
                        def _(low=low, number=number):
                            if low == 0:
                                acc[...] = dot_of(low, number)
                            else:
                                acc[...] += dot_of(low, number)

                blocks = [acc[:, m * size : (m + 1) * size] for m in range(slots)]
                if extra is not None:
                    scale = scales(extra_ref.at[g], slots, size)
                    blocks = [b + decode(extra_ref.at[g], scale, m, size) for m, b in enumerate(blocks)]
                encode(outs[0].at[g] if joined else outs[t].at[i], blocks)
                return carry

            lax.fori_loop(0, n, one, 0)

    if joined:
        out_shape = [jax.ShapeDtypeStruct((rows, height, size), jnp.int16)]
    else:
        out_shape = [jax.ShapeDtypeStruct((n, height, size), jnp.int16)] * parts
    operands = [table, values, *lefts] + ([] if extra is None else [extra])
    out = pl.pallas_call(
        kernel,
        out_shape=out_shape,
        in_specs=[SCALARS] + [NEAR] * (len(operands) - 1),
        out_specs=[NEAR] * len(out_shape),
        scratch_shapes=[pltpu.VMEM((size, slots * size), jnp.float32)],
        compiler_params=pltpu.CompilerParams(vmem_limit_bytes=VMEM_BYTES),
        cost_estimate=pl.CostEstimate(
            flops=2 * rows * terms * slots * size**3,
            bytes_accessed=rows * terms * (slots + 1) * size * size * 2,
            transcendentals=0,
        ),
        name="product",
    )(*operands)
    return out[0] if joined else out


def finish(received, own, flags, where, depths, first, count, before=None):
    parts = len(received)
    n, _, size = received[0].shape
    slots = own.shape[1]

    def kernel(flag_ref, where_ref, own_ref, *refs):
        got, out_ref = refs[:parts], refs[-1]
        i = pl.program_id(0)
        flag = flag_ref[(where_ref[0] * depths + where_ref[1]) * count + first + i]
        scale = [scales(g.at[i], slots, size) for g in got]
        for m in range(slots):
            total = decode(got[0].at[i], scale[0], m, size)
            for p in range(1, parts):
                total = total + decode(got[p].at[i], scale[p], m, size)
            mine = own_ref[i, m].astype(jnp.float32)
            out_ref[0, m] = jnp.where(flag == 1, total, 2.0 * mine - total).astype(out_ref.dtype)

    in_specs = [NEAR] * (parts + 1)
    operands = [flags, where, own, *received]
    if before is not None:
        in_specs.append(HERE)
        operands.append(before)
    return pl.pallas_call(
        kernel,
        out_shape=jax.ShapeDtypeStruct((count, slots, size, size), own.dtype),
        grid_spec=pltpu.PrefetchScalarGridSpec(
            num_scalar_prefetch=2,
            grid=(n,),
            in_specs=in_specs,
            out_specs=pl.BlockSpec((1, slots, size, size), lambda i, *_: (first + i, 0, 0, 0)),
        ),
        compiler_params=pltpu.CompilerParams(vmem_limit_bytes=VMEM_BYTES),
        input_output_aliases={} if before is None else {len(operands) - 1: 0},
        name="finish",
    )(*operands)


def inner(values, pattern, branch_flag):
    parts, depths, panels = lax.axis_size("row"), lax.axis_size("depth"), lax.axis_size("col")
    row, depth, z = lax.axis_index("row"), lax.axis_index("depth"), lax.axis_index("col")
    rows_here, slots, _, _ = values.shape
    count = branch_flag.shape[0] // (parts * depths)
    stride = rows_here // count
    panel_cols = rows_here * parts * depths // panels
    per_part = panels // parts
    chunks = chunks_of(count)
    across = [[(i, i ^ t) for i in range(parts)] for t in range(parts)]
    stops = [*range(0, 1), *range(1, panels, 2), *range(panels - 2 + panels % 2, 0, -2)]
    ring = list(zip(stops, stops[1:] + stops[:1]))
    where = jnp.stack([row, depth, z]).astype(jnp.int32)

    own = [values[a * stride : (a + n - 1) * stride + 1 : stride] for a, n in chunks]
    every = lax.all_to_all(
        jnp.broadcast_to(pattern[None, ::stride], (parts * panels * depths, count, slots)),
        ("row", "col", "depth"), split_axis=0, concat_axis=0, tiled=True,
    )
    tables, near = make_tables(
        where, every.reshape(-1), pattern.reshape(-1), values,
        (parts, panels, depths, count, slots, rows_here, panel_cols), chunks,
    )

    held = [[x] for x in own]
    for _ in range(panels - 1):
        for c in range(len(chunks)):
            held[c].append(lax.ppermute(held[c][-1], "col", ring))

    out = None
    lefts = []
    for c in range(len(chunks)):
        picked = gather_panels(held[c], where, parts, per_part)
        got = [picked[0]]
        for t in range(1, parts):
            got.append(lax.ppermute(picked[t], "row", across[t]))
        lefts.append(got)

    base = [sum(parts * m for _, m in chunks[:c]) for c in range(len(chunks))]
    per_depth = parts * count
    for c, (first, n) in enumerate(chunks):
        extra = None
        for s in range(1, depths):
            here = []
            for t in range(parts):
                here.append(
                    lax.ppermute(lefts[c][t], "depth", [((i + s) % depths, i) for i in range(depths)])
                )
            part = product(here, near, tables, s * per_depth + base[c], joined=True)
            back = lax.ppermute(part, "depth", [(i, (i + s) % depths) for i in range(depths)])
            assert extra is None
            extra = back
        mine = product(lefts[c], near, tables, base[c], extra=extra)
        summed = [mine[0]]
        for t in range(1, parts):
            summed.append(lax.ppermute(mine[t], "row", across[t]))
        out = finish(summed, own[c], branch_flag, where, depths, first, count, before=out)
    return out


def solution(mesh):
    in_specs = (P(("row", "depth"), "col", None, None), P(("row", "depth"), "col"), P())
    out_specs = P(("row", "depth"), "col", None, None)
    return jax.shard_map(inner, mesh=mesh, in_specs=in_specs, out_specs=out_specs, check_vma=False)
```
